512 devices in a mesh: opt: 128 (over y, z, core), layer: 4 (over x).
Axes of the slice: x: 4, y: 8, z: 8, core: 2. Of those that a mesh axis runs over, the one named last changes fastest.
Arguments:
- momentum: bfloat16 [4, 128, 1024, 512], P('layer', None, 'opt'), may hold values from -4000 to 4000
- weights: bfloat16 [4, 128, 1024, 512], P('layer', None, 'opt'), may hold values from -6 to 6
Outputs:
- new_weights: bfloat16 [4, 128, 1024, 512], P('layer', None, 'opt')
The draws below stay inside these ranges and needn't reach their ends.
All inputs are finite; a program needn't handle non-finite values.
Results may differ from the reference program's by a relative error of at most 0.0041.
Values may be sent and summed in bfloat16 or wider, within the bound.
A program may use at most 64 MiB of HBM per device.

```python
import math
import jax
import jax.numpy as jnp
from jax import lax

D = 1024
FF = 512
ITERS = 3
EXPERTS = 128
LAYERS = 4


def draw_momentum(key, part):
    subkeys = jax.random.split(key, 3)
    full_shape = (LAYERS, EXPERTS, D, FF)
    row_scale = jnp.exp(jax.random.uniform(subkeys[0], (LAYERS, EXPERTS, D, 1), jnp.float32, 0.0, math.log(10.0)))
    col_scale = jnp.exp(jax.random.uniform(subkeys[1], (LAYERS, EXPERTS, 1, FF), jnp.float32, 0.0, math.log(10.0)))
    layer_ramp = lax.broadcasted_iota(jnp.float32, (LAYERS, 1, 1, 1), 0) / max(LAYERS - 1, 1)
    entries = jax.random.truncated_normal(subkeys[2], -4.0, 4.0, full_shape, jnp.float32)
    layer_scale = 1.0 + 2.0 * layer_ramp
    return (entries * row_scale * col_scale * layer_scale).astype(jnp.bfloat16)


def levels(key, dims, cuts, low, high):
    level = 1.0
    for position, shards_of in cuts:
        heights = jax.random.uniform(jax.random.fold_in(jax.random.fold_in(key, 6), position), (shards_of,), jnp.float32, low / len(cuts), high / len(cuts))
        level = level * jnp.repeat(jnp.exp(heights), dims[position] // shards_of).reshape((-1,) + (1,) * (len(dims) - 1 - position))
    return level


def scatter_about(rng, extent, deviation, reach, shards=(), held_as=jnp.bfloat16):
    values = jax.random.normal(rng, extent, jnp.float32) * deviation
    if len(shards) > 0:
        values = levels(rng, extent, shards, -0.22, 0.18) * values
    return jnp.clip(values, min=-reach, max=reach).astype(held_as)


def setup_inputs(seed: int = 0) -> dict:
    seeds = jax.random.split(jax.random.key(seed), 3)
    momentum = draw_momentum(jax.random.fold_in(seeds[2], 71), 0)
    weights = scatter_about(seeds[1], (LAYERS, EXPERTS, D, FF), 1.0, 6.0, ((0, 4), (2, 128)))
    return {"momentum": momentum, "weights": weights}


first_coef = 3.4445
second_coef = -4.775
third_coef = 2.0315
epsilon = 1e-06
step_rate = 0.5
decay_rate = 0.1

def newton(gram_sum, trace_sum):
    highest = lax.Precision.HIGHEST
    identity_matrix = jnp.eye(FF, dtype=jnp.float32)
    current = gram_sum / (trace_sum + epsilon)
    accum = identity_matrix
    for iteration in range(ITERS):
        squared = jnp.dot(current, current, precision=highest)
        polynomial = first_coef * identity_matrix + second_coef * current + third_coef * squared
        accum = jnp.dot(accum, polynomial, precision=highest)
        if iteration + 1 < ITERS:
            current = jnp.dot(jnp.dot(current, polynomial, precision=highest), polynomial, precision=highest)
    return accum

def reference(momentum, weights):

    def one_expert(expert):
        stacked = lax.dynamic_index_in_dim(momentum, expert, 1, keepdims=False)
        plates = lax.dynamic_index_in_dim(weights, expert, 1, keepdims=False)
        gram_sum = jnp.zeros((FF, FF), jnp.float32)
        for layer_index in range(LAYERS):
            gram_sum = gram_sum + jnp.dot(stacked[layer_index].T, stacked[layer_index], preferred_element_type=jnp.float32)
        trace_sum = jnp.trace(gram_sum)
        accum = newton(gram_sum, trace_sum)
        factor = (accum * jnp.sqrt(LAYERS * D / (trace_sum + epsilon))).astype(jnp.bfloat16)
        results = []
        for layer_index in range(LAYERS):
            update = jnp.dot(stacked[layer_index], factor, preferred_element_type=jnp.float32).astype(jnp.bfloat16)
            update = lax.optimization_barrier(update)
            shrink = 1.0 - step_rate * decay_rate
            fresh = shrink * plates[layer_index].astype(jnp.float32) - step_rate * update.astype(jnp.float32)
            results.append(fresh.astype(jnp.bfloat16))
        return jnp.stack(results)
    mapped = lax.map(one_expert, jnp.arange(EXPERTS, dtype=jnp.int32))
    return jnp.swapaxes(mapped, 0, 1)
```

```python
import jax
import jax.numpy as jnp
from jax import lax
from jax.sharding import Mesh
from jax.sharding import PartitionSpec as P

ITERS = 3
OPT = ("opt_0", "opt_1", "opt_2")


first_coef = 3.4445
second_coef = -4.775
third_coef = 2.0315
epsilon = 1e-06
step_rate = 0.5
decay_rate = 0.1


def sent_to_all(shard, axis):
    size = lax.axis_size(axis)
    return lax.all_to_all(
        jnp.broadcast_to(shard[None], (size, *shard.shape)), axis, 0, 0, tiled=True
    )


def of_everyone(shard, axis):
    size = lax.axis_size(axis)
    dims = shard.shape
    slabs = shard.reshape(size, dims[-2] // size, dims[-1])
    mine = lax.all_to_all(slabs, axis, 0, 0, tiled=True).sum(axis=0)
    return sent_to_all(mine, axis).reshape(dims)


def in_blocks(shard, dim, size):
    dims = shard.shape
    tiles = shard.reshape(*dims[:dim], size, dims[dim] // size, *dims[dim + 1 :])
    return jnp.moveaxis(tiles, dim, 0)


def laid_out(tiles, dim):
    tiles = jnp.moveaxis(tiles, 0, dim)
    dims = tiles.shape
    return tiles.reshape(*dims[:dim], dims[dim] * dims[dim + 1], *dims[dim + 2 :])


def turned_blocks(tiles, axes, order):
    inside = tiles.shape[1:]
    filled = tiles.reshape(*(lax.axis_size(a) for a in axes), *inside)
    for k in order:
        filled = lax.all_to_all(filled, axes[k], k, k, tiled=True)
    return filled.reshape(-1, *inside)


def two_step_exchange(shard, groups, order, split_dim, concat_dim):
    size = lax.axis_size(groups[0]) * lax.axis_size(groups[1])
    tiles = in_blocks(shard, split_dim, size)
    return laid_out(turned_blocks(tiles, groups, order), concat_dim)


def batched(first_matrix, second_matrix):
    return jnp.einsum("erk,ekc->erc", first_matrix, second_matrix, precision=lax.Precision.HIGH)


def identity_rows(row_count, gram_order):
    column_ids = lax.broadcasted_iota(jnp.int32, (row_count, gram_order), 1)
    row_ids = lax.broadcasted_iota(jnp.int32, (row_count, gram_order), 0)
    return (column_ids == row_ids).astype(jnp.float32)[None]


def newton_whole(gram_sum, trace_sum):
    identity_matrix = identity_rows(gram_sum.shape[1], gram_sum.shape[2])
    current = gram_sum / (trace_sum + epsilon)[:, None, None]
    accum = jnp.broadcast_to(identity_matrix, current.shape)
    for iteration in range(ITERS):
        squared = batched(current, current)
        polynomial = first_coef * identity_matrix + second_coef * current + third_coef * squared
        accum = batched(accum, polynomial)
        if iteration + 1 < ITERS:
            current = batched(batched(current, polynomial), polynomial)
    return accum


def on_device(momentum, weights):
    regrouped = lax.all_to_all(momentum, OPT, split_axis=1, concat_axis=2, tiled=True)[0]
    layers = lax.axis_size("layer")
    matrix_rows = regrouped.shape[1]
    gram_local = lax.dot_general(
        regrouped, regrouped, (((1,), (1,)), ((0,), (0,))), preferred_element_type=jnp.float32
    )
    gram_sum = of_everyone(gram_local, "layer")
    trace_sum = jnp.trace(gram_sum, axis1=1, axis2=2)
    accum = newton_whole(gram_sum, trace_sum)
    factor = (accum * jnp.sqrt(layers * matrix_rows / (trace_sum + epsilon))[:, None, None]).astype(
        jnp.bfloat16
    )
    update = lax.dot_general(
        regrouped, factor, (((2,), (1,)), ((0,), (0,))), preferred_element_type=jnp.float32
    )
    update = update.astype(jnp.bfloat16)[None]
    returned = two_step_exchange(update, (("opt_0", "opt_1"), "opt_2"), (1, 0), 2, 1)
    shrink = 1.0 - step_rate * decay_rate
    return (shrink * weights.astype(jnp.float32) - step_rate * returned.astype(jnp.float32)).astype(
        jnp.bfloat16
    )


def solution(mesh):
    split = Mesh(
        mesh.devices.reshape(8, 8, 2, mesh.shape["layer"]), ("opt_0", "opt_1", "opt_2", "layer")
    )
    in_specs = (P("layer", None, OPT, None), P("layer", None, OPT, None))
    out_specs = P("layer", None, OPT, None)
    return jax.shard_map(
        on_device, mesh=split, in_specs=in_specs, out_specs=out_specs, check_vma=False
    )
```

```python
import functools

import jax
import jax.numpy as jnp
from jax import lax
from jax.experimental import pallas as pl
from jax.experimental.pallas import tpu as pltpu
from jax.sharding import PartitionSpec as P

ITERS = 3
MESH = pl.DeviceIdType.MESH
DMA = pltpu.SemaphoreType.DMA

first_coef = 3.4445
second_coef = -4.775
third_coef = 2.0315
epsilon = 1e-06
step_rate = 0.5
decay_rate = 0.1
shrink = 1.0 - step_rate * decay_rate

B = 128


def signed(k):
    half = (k + 1) // 2
    return jnp.where(lax.rem(k, 2) == 1, half, lax.rem(8 - half, 8))


def target(y, z, k):
    return lax.rem(y + signed(k // 8), 8) * 8 + lax.rem(z + signed(lax.rem(k, 8)), 8)


def dot(a, b):
    return jnp.dot(a, b, preferred_element_type=jnp.float32)


def split(value, ref, cols):
    high = value.astype(jnp.bfloat16)
    ref[0, :, cols] = high
    ref[1, :, cols] = (value - high.astype(jnp.float32)).astype(jnp.bfloat16)


def product(a_ref, b_ref, finish, width=256):
    n = a_ref.shape[1]
    left = jnp.concatenate([a_ref[0], a_ref[1], a_ref[0]], axis=1)
    for j in range(n // width):
        cols = pl.ds(j * width, width)
        right = jnp.concatenate([b_ref[0, :, cols], b_ref[0, :, cols], b_ref[1, :, cols]], axis=0)
        finish(dot(left, right), cols, j * width)


def unit(rows, width, start):
    r = lax.broadcasted_iota(jnp.int32, (rows, width), 0)
    c = lax.broadcasted_iota(jnp.int32, (rows, width), 1)
    return (r == c + start).astype(jnp.float32)


def step_kernel(m_ref, w_ref, o_ref, inb, upd, ub, wv, mat, g, ra, g2, rb, cur, cs, ps, qs, acs, fac,
                in_send, in_recv, w_sem, x_send, x_recv, out_send, out_recv):
    opt, x = lax.axis_index("opt"), lax.axis_index("layer")
    layers = 4
    chip, c = opt // 2, lax.rem(opt, 2)
    y, z = chip // 8, lax.rem(chip, 8)
    near = (x + 1 - 2 * lax.rem(x, 2), layers - 1 - x)

    pltpu.make_async_copy(m_ref.at[chip, c], inb.at[chip, c], in_recv).start()
    pltpu.make_async_copy(w_ref, wv, w_sem).start()

    barrier = pltpu.get_barrier_semaphore()

    def greet(k, carry):
        pl.semaphore_signal(barrier, inc=1, device_id=(lax.rem(opt + k, 128), x), device_id_type=MESH)
        return carry

    lax.fori_loop(1, 128, greet, 0)
    for other in near:
        pl.semaphore_signal(barrier, inc=1, device_id=(opt, other), device_id_type=MESH)
    pl.semaphore_wait(barrier, 129)

    for core in range(2):
        def give(k, carry):
            t = target(y, z, k)

            @pl.when((t * 2 + core) != opt)
            def _():
                pltpu.make_async_remote_copy(
                    m_ref.at[t, core], inb.at[chip, c], in_send, in_recv,
                    device_id=(t * 2 + core, x), device_id_type=MESH,
                ).start()
            return carry

        lax.fori_loop(0, 64, give, 0)
    pltpu.make_async_copy(inb, inb, in_recv).wait()

    def lay(i, carry):
        rows = inb[pl.ds(i * 4, 4)].astype(jnp.float32).reshape(64, 512)
        mat[pl.ds(pl.multiple_of(i * 64, 64), 64), :] = rows.astype(jnp.bfloat16)
        return carry

    lax.fori_loop(0, 16, lay, 0)

    def gram(lo, hi, start):
        return lax.dot_general(mat[:, lo:hi], mat[:, start:], (((0,), (0,)), ((), ())), preferred_element_type=jnp.float32)

    top = gram(0, 256, 0)
    g[0, :, 0:512] = top[0:128]
    g[1, :, 0:384] = top[128:256, 128:]
    low = gram(256, 512, 256)
    g[1, :, 384:640] = low[0:128]
    g[0, :, 512:640] = low[128:256, 128:]

    def exchange(src, dst, stage, half):
        other = near[(stage + half) % 2]
        return pltpu.make_async_remote_copy(
            src.at[half], dst.at[half], x_send.at[stage, half], x_recv.at[stage, half],
            device_id=(opt, other), device_id_type=MESH,
        )

    for half in range(2):
        exchange(g, ra, 0, half).start()
    for half in range(2):
        exchange(g, ra, 0, half).wait_recv()
        g2[half] = g[half] + ra[half]
        exchange(g2, rb, 1, half).start()
    for half in range(2):
        exchange(g2, rb, 1, half).wait_recv()

    where = {0: (0, 0), 1: (1, 0), 2: (1, 384), 3: (0, 512)}

    def block(i, j):
        half, base = where[i]
        cols = slice(base + (j - i) * B, base + (j - i + 1) * B)
        return g2[half, :, cols] + rb[half, :, cols]

    eye = unit(B, B, 0)
    diagonal = jnp.zeros((B, B), jnp.float32)
    for i in range(4):
        for j in range(i, 4):
            blk = block(i, j)
            cur[i * B:(i + 1) * B, j * B:(j + 1) * B] = blk
            if i == j:
                diagonal = diagonal + blk * eye
            else:
                cur[j * B:(j + 1) * B, i * B:(i + 1) * B] = blk.T
    trace = jnp.sum(jnp.sum(diagonal, axis=0, keepdims=True), axis=1, keepdims=True) + epsilon
    scale = 1.0 / trace
    for j in range(2):
        cols = pl.ds(j * 256, 256)
        value = cur[:, cols] * scale
        cur[:, cols] = value
        split(value, cs, cols)

    def poly(panel, cols, start):
        value = first_coef * unit(512, 256, start) + second_coef * cur[:, cols] + third_coef * panel
        split(value, ps, cols)
        return value

    def keep_current(panel, cols, start):
        cur[:, cols] = panel
        split(panel, cs, cols)

    product(cs, cs, poly)
    product(cs, ps, lambda v, cols, start: split(v, qs, cols))
    product(qs, ps, keep_current)
    for h in range(2):
        acs[h] = ps[h]
    product(cs, cs, poly)
    product(acs, ps, lambda v, cols, start: split(v, acs2(acs), cols))
    product(cs, ps, lambda v, cols, start: split(v, qs, cols))
    product(qs, ps, keep_current)
    product(cs, cs, poly)
    root = jnp.sqrt((layers * 1024) / trace)

    def last(v, cols, start):
        fac[:, cols] = (v * root).astype(jnp.bfloat16)

    product(acs2(acs), ps, last)

    def update(i, carry):
        rows = mat[pl.ds(pl.multiple_of(i * 256, 256), 256), :]
        upd[pl.ds(i * 16, 16)] = dot(rows, fac[...]).reshape(16, 2, 8, 512).astype(jnp.bfloat16)
        return carry

    lax.fori_loop(0, 4, update, 0)

    pltpu.make_async_copy(upd.at[chip, c], ub.at[chip, c], out_recv.at[c]).start()

    def give_back(k, carry):
        t = target(y, z, k)
        for core in range(2):
            @pl.when((t * 2 + core) != opt)
            def _(core=core):
                pltpu.make_async_remote_copy(
                    upd.at[t, core], ub.at[chip, c], out_send, out_recv.at[c],
                    device_id=(t * 2 + core, x), device_id_type=MESH,
                ).start()
        return carry

    lax.fori_loop(0, 64, give_back, 0)

    pltpu.make_async_copy(w_ref, wv, w_sem).wait()
    for core in range(2):
        pltpu.make_async_copy(ub.at[:, core], ub.at[:, core], out_recv.at[core]).wait()

        def finish(i, carry):
            rows = pl.ds(i * 8, 8)
            old = wv[rows, core].astype(jnp.float32)
            o_ref[rows, core] = (shrink * old - step_rate * ub[rows, core].astype(jnp.float32)).astype(jnp.bfloat16)
            return carry

        lax.fori_loop(0, 8, finish, 0)

    sent = pl.ds(0, 63)
    for sem, buf in ((in_send, inb), (out_send, ub)):
        pltpu.make_async_copy(buf.at[sent], buf.at[sent], sem).wait()
        pltpu.make_async_copy(buf.at[0, 0], buf.at[0, 0], sem).wait()
    for half in range(2):
        exchange(g, ra, 0, half).wait_send()
        exchange(g2, rb, 1, half).wait_send()


class acs2:
    def __init__(self, ref):
        self.ref = ref
        self.shape = ref.shape

    def __getitem__(self, at):
        at = at if isinstance(at, tuple) else (at,)
        return self.ref[(at[0] + 2, *at[1:])]

    def __setitem__(self, at, value):
        self.ref[(at[0] + 2, *at[1:])] = value


def on_device(momentum, weights):
    places = (64, 2, 8, 512)
    bf, f4 = jnp.bfloat16, jnp.float32
    out = pl.pallas_call(
        step_kernel,
        name="orthogonal_step",
        out_shape=jax.ShapeDtypeStruct(places, bf),
        in_specs=[pl.BlockSpec(memory_space=pl.ANY)] * 2,
        out_specs=pl.BlockSpec(memory_space=pltpu.VMEM),
        scratch_shapes=[
            *[pltpu.VMEM(places, bf)] * 4,
            pltpu.VMEM((1024, 512), bf),
            *[pltpu.VMEM((2, B, 640), f4)] * 4,
            pltpu.VMEM((512, 512), f4),
            *[pltpu.VMEM((2, 512, 512), bf)] * 3,
            pltpu.VMEM((4, 512, 512), bf),
            pltpu.VMEM((512, 512), bf),
            DMA, DMA, DMA, DMA((2, 2)), DMA((2, 2)), DMA, DMA((2,)),
        ],
        compiler_params=pltpu.CompilerParams(collective_id=0, has_side_effects=True, vmem_limit_bytes=56 * 2**20),
    )(momentum.reshape(places), weights.reshape(places))
    return out.reshape(momentum.shape)


def solution(mesh):
    spec = P("layer", None, "opt", None)
    return jax.shard_map(on_device, mesh=mesh, in_specs=(spec, spec), out_specs=spec, check_vma=False)
```

```python
import functools

import jax
import jax.numpy as jnp
from jax import lax
from jax.experimental import pallas as pl
from jax.experimental.pallas import tpu as pltpu
from jax.sharding import PartitionSpec as P

ITERS = 3
MESH = pl.DeviceIdType.MESH
DMA = pltpu.SemaphoreType.DMA

first_coef = 3.4445
second_coef = -4.775
third_coef = 2.0315
epsilon = 1e-06
step_rate = 0.5
decay_rate = 0.1
shrink = 1.0 - step_rate * decay_rate

B = 128
WINDOW = 3
HELD = 6


def signed(k):
    half = (k + 1) // 2
    return jnp.where(lax.rem(k, 2) == 1, half, lax.rem(8 - half, 8))


def target(y, z, odd, k):
    row, j = k // 4, lax.rem(k, 4)
    dy = signed(row)
    turn = lax.rem(y + z + dy + odd, 2)
    dz = signed(jnp.where(turn == 1, j + j // 2 * 2 + 1, j + (j + 1) // 2 * 2))
    return lax.rem(y + dy, 8) * 8 + lax.rem(z + dz, 8)


def dot(a, b):
    return jnp.dot(a, b, preferred_element_type=jnp.float32)


def split(value, ref, cols):
    high = value.astype(jnp.bfloat16)
    ref[0, :, cols] = high
    ref[1, :, cols] = (value - high.astype(jnp.float32)).astype(jnp.bfloat16)


def product(a_ref, b_ref, finish, width=256):
    n = a_ref.shape[1]
    left = jnp.concatenate([a_ref[0], a_ref[1], a_ref[0]], axis=1)
    for j in range(n // width):
        cols = pl.ds(j * width, width)
        right = jnp.concatenate([b_ref[0, :, cols], b_ref[0, :, cols], b_ref[1, :, cols]], axis=0)
        finish(dot(left, right), cols, j * width)


def unit(rows, width, start):
    r = lax.broadcasted_iota(jnp.int32, (rows, width), 0)
    c = lax.broadcasted_iota(jnp.int32, (rows, width), 1)
    return (r == c + start).astype(jnp.float32)


def step_kernel(m_ref, ub, inb, upd, spare, mat, g, ra, g2, rb, cur, cs, ps, qs, acs, fac,
                own, in_send, in_recv, x_send, x_recv, out_send, out_recv):
    opt, x = lax.axis_index("opt"), lax.axis_index("layer")
    layers = 4
    chip, c = opt // 2, lax.rem(opt, 2)
    y, z = chip // 8, lax.rem(chip, 8)
    near = (x + 1 - 2 * lax.rem(x, 2), layers - 1 - x)

    pltpu.make_async_copy(m_ref.at[opt], inb.at[opt], own).start()
    pltpu.make_async_copy(m_ref.at[opt], spare, in_send.at[2 * (2 * c + lax.rem(y + z, 2))]).start()

    barrier = pltpu.get_barrier_semaphore()

    def greet(k, carry):
        pl.semaphore_signal(barrier, inc=1, device_id=(lax.rem(opt + k, 128), x), device_id_type=MESH)
        return carry

    lax.fori_loop(1, 128, greet, 0)
    for other in near:
        pl.semaphore_signal(barrier, inc=1, device_id=(opt, other), device_id_type=MESH)
    pl.semaphore_wait(barrier, 129)

    def give(group):
        def one(k, carry):
            d = target(y, z, lax.rem(group // 2, 2), k) * 2 + group // 4

            @pl.when(d != opt)
            def _():
                pltpu.make_async_remote_copy(
                    m_ref.at[d], inb.at[opt], in_send.at[group], in_recv,
                    device_id=(d, x), device_id_type=MESH,
                ).start()
            return carry

        start = lax.rem(group, 2) * 16
        lax.fori_loop(start, start + 16, one, 0)

    def given(group):
        sent = inb.at[pl.ds(0, 16)]
        pltpu.make_async_copy(sent, sent, in_send.at[group]).wait()

    def give_next(group, carry):
        given(group - WINDOW)
        give(group)
        return carry

    def first(group, carry):
        give(group)
        return carry

    lax.fori_loop(0, WINDOW, first, 0)
    lax.fori_loop(WINDOW, HELD, give_next, 0)

    @pl.when(c == 1)
    def _():
        lax.fori_loop(HELD, 8, give_next, 0)

    pltpu.make_async_copy(inb.at[pl.ds(0, 127)], inb.at[pl.ds(0, 127)], in_recv).wait()
    pltpu.make_async_copy(inb.at[0], inb.at[0], own).wait()

    def lay(i, carry):
        rows = inb[pl.ds(i * 8, 8)].astype(jnp.float32).reshape(64, 512)
        mat[pl.ds(pl.multiple_of(i * 64, 64), 64), :] = rows.astype(jnp.bfloat16)
        return carry

    lax.fori_loop(0, 16, lay, 0)

    def gram(lo, hi, start):
        return lax.dot_general(mat[:, lo:hi], mat[:, start:], (((0,), (0,)), ((), ())), preferred_element_type=jnp.float32)

    top = gram(0, 256, 0)
    g[0, :, 0:512] = top[0:128]
    g[1, :, 0:384] = top[128:256, 128:]
    low = gram(256, 512, 256)
    g[1, :, 384:640] = low[0:128]
    g[0, :, 512:640] = low[128:256, 128:]

    def exchange(src, dst, stage, half):
        other = near[(stage + half) % 2]
        return pltpu.make_async_remote_copy(
            src.at[half], dst.at[half], x_send.at[stage, half], x_recv.at[stage, half],
            device_id=(opt, other), device_id_type=MESH,
        )

    for half in range(2):
        exchange(g, ra, 0, half).start()

    @pl.when(c == 0)
    def _():
        lax.fori_loop(HELD, 8, give_next, 0)

    for half in range(2):
        exchange(g, ra, 0, half).wait_recv()
        g2[half] = g[half] + ra[half]
        exchange(g2, rb, 1, half).start()
    for half in range(2):
        exchange(g2, rb, 1, half).wait_recv()

    where = {0: (0, 0), 1: (1, 0), 2: (1, 384), 3: (0, 512)}

    def block(i, j):
        half, base = where[i]
        cols = slice(base + (j - i) * B, base + (j - i + 1) * B)
        return g2[half, :, cols] + rb[half, :, cols]

    eye = unit(B, B, 0)
    diagonal = jnp.zeros((B, B), jnp.float32)
    for i in range(4):
        for j in range(i, 4):
            blk = block(i, j)
            cur[i * B:(i + 1) * B, j * B:(j + 1) * B] = blk
            if i == j:
                diagonal = diagonal + blk * eye
            else:
                cur[j * B:(j + 1) * B, i * B:(i + 1) * B] = blk.T
    trace = jnp.sum(jnp.sum(diagonal, axis=0, keepdims=True), axis=1, keepdims=True) + epsilon
    scale = 1.0 / trace
    for j in range(2):
        cols = pl.ds(j * 256, 256)
        value = cur[:, cols] * scale
        cur[:, cols] = value
        split(value, cs, cols)

    def poly(panel, cols, start):
        value = first_coef * unit(512, 256, start) + second_coef * cur[:, cols] + third_coef * panel
        split(value, ps, cols)
        return value

    def keep_current(panel, cols, start):
        cur[:, cols] = panel
        split(panel, cs, cols)

    product(cs, cs, poly)
    product(cs, ps, lambda v, cols, start: split(v, qs, cols))
    product(qs, ps, keep_current)
    for h in range(2):
        acs[h] = ps[h]
    product(cs, cs, poly)
    product(acs, ps, lambda v, cols, start: split(v, acs2(acs), cols))
    product(cs, ps, lambda v, cols, start: split(v, qs, cols))
    product(qs, ps, keep_current)
    product(cs, cs, poly)
    root = jnp.sqrt((layers * 1024) / trace)

    def last(v, cols, start):
        fac[:, cols] = (v * root).astype(jnp.bfloat16)

    product(acs2(acs), ps, last)

    def update(i, carry):
        rows = mat[pl.ds(pl.multiple_of(i * 256, 256), 256), :]
        upd[pl.ds(i * 32, 32)] = dot(rows, fac[...]).reshape(32, 8, 512).astype(jnp.bfloat16)
        return carry

    lax.fori_loop(0, 4, update, 0)

    pltpu.make_async_copy(upd.at[opt], ub.at[opt], own).start()

    def give_back(k, carry):
        d = target(y, z, lax.rem(k // 2, 2), k // 4) * 2 + lax.rem(k, 2)

        @pl.when(d != opt)
        def _():
            pltpu.make_async_remote_copy(
                upd.at[d], ub.at[opt], out_send, out_recv,
                device_id=(d, x), device_id_type=MESH,
            ).start()
        return carry

    lax.fori_loop(0, 128, give_back, 0)

    def sent(group, carry):
        given(group)
        return carry

    lax.fori_loop(8 - WINDOW, 8, sent, 0)
    for half in range(2):
        exchange(g, ra, 0, half).wait_send()
        exchange(g2, rb, 1, half).wait_send()
    others = pl.ds(0, 127)
    pltpu.make_async_copy(upd.at[others], upd.at[others], out_send).wait()
    pltpu.make_async_copy(ub.at[others], ub.at[others], out_recv).wait()
    pltpu.make_async_copy(upd.at[0], upd.at[0], own).wait()


class acs2:
    def __init__(self, ref):
        self.ref = ref
        self.shape = ref.shape

    def __getitem__(self, at):
        at = at if isinstance(at, tuple) else (at,)
        return self.ref[(at[0] + 2, *at[1:])]

    def __setitem__(self, at, value):
        self.ref[(at[0] + 2, *at[1:])] = value


def on_device(momentum, weights):
    places = (128, 8, 512)
    bf, f4 = jnp.bfloat16, jnp.float32
    update = pl.pallas_call(
        step_kernel,
        name="orthogonal_update",
        out_shape=jax.ShapeDtypeStruct(places, bf),
        in_specs=[pl.BlockSpec(memory_space=pl.ANY)],
        out_specs=pl.BlockSpec(memory_space=pl.ANY),
        scratch_shapes=[
            *[pltpu.VMEM(places, bf)] * 2,
            pltpu.VMEM((8, 512), bf),
            pltpu.VMEM((1024, 512), bf),
            *[pltpu.VMEM((2, B, 640), f4)] * 4,
            pltpu.VMEM((512, 512), f4),
            *[pltpu.VMEM((2, 512, 512), bf)] * 3,
            pltpu.VMEM((4, 512, 512), bf),
            pltpu.VMEM((512, 512), bf),
            DMA, DMA((8,)), DMA, DMA((2, 2)), DMA((2, 2)), DMA, DMA,
        ],
        compiler_params=pltpu.CompilerParams(collective_id=0, has_side_effects=True, vmem_limit_bytes=56 * 2**20),
    )(momentum.reshape(places))
    update = update.reshape(weights.shape).astype(jnp.float32)
    return (shrink * weights.astype(jnp.float32) - step_rate * update).astype(jnp.bfloat16)


def solution(mesh):
    spec = P("layer", None, "opt", None)
    return jax.shard_map(on_device, mesh=mesh, in_specs=(spec, spec), out_specs=spec, check_vma=False)
```

```python
import functools

import jax
import jax.numpy as jnp
from jax import lax
from jax.experimental import pallas as pl
from jax.experimental.pallas import tpu as pltpu
from jax.sharding import PartitionSpec as P

ITERS = 3
MESH = pl.DeviceIdType.MESH
DMA = pltpu.SemaphoreType.DMA

first_coef = 3.4445
second_coef = -4.775
third_coef = 2.0315
epsilon = 1e-06
step_rate = 0.5
decay_rate = 0.1
shrink = 1.0 - step_rate * decay_rate

B = 128


TURNS = (4, 5, 3, 6, 2, 7, 1, 0)


def turn_of(k):
    half = (8 - k) // 2
    return jnp.where(lax.rem(k, 2) == 1, 8 - half, half)


def ahead(at, turn):
    there = at + turn
    return jnp.where(there >= 8, there - 8, there)


def dot(a, b):
    return jnp.dot(a, b, preferred_element_type=jnp.float32)


def split(value, ref, cols):
    high = value.astype(jnp.bfloat16)
    ref[0, :, cols] = high
    ref[1, :, cols] = (value - high.astype(jnp.float32)).astype(jnp.bfloat16)


def product(a_ref, b_ref, finish, width=256):
    n = a_ref.shape[1]
    left = jnp.concatenate([a_ref[0], a_ref[1], a_ref[0]], axis=1)
    for j in range(n // width):
        cols = pl.ds(j * width, width)
        right = jnp.concatenate([b_ref[0, :, cols], b_ref[0, :, cols], b_ref[1, :, cols]], axis=0)
        finish(dot(left, right), cols, j * width)


def unit(rows, width, start):
    r = lax.broadcasted_iota(jnp.int32, (rows, width), 0)
    c = lax.broadcasted_iota(jnp.int32, (rows, width), 1)
    return (r == c + start).astype(jnp.float32)


def step_kernel(m_ref, ub, inb, upd, mat, g, ra, g2, rb, cur, cs, ps, qs, acs, fac,
                own, in_send, in_recv, x_send, x_recv, out_send, out_recv):
    opt, x = lax.axis_index("opt"), lax.axis_index("layer")
    layers = 4
    chip, c = opt // 2, lax.rem(opt, 2)
    y, z = chip // 8, lax.rem(chip, 8)
    near = (x + 1 - 2 * lax.rem(x, 2), layers - 1 - x)

    pltpu.make_async_copy(m_ref.at[opt], inb.at[opt], own).start()

    barrier = pltpu.get_barrier_semaphore()

    def greet(k, carry):
        pl.semaphore_signal(barrier, inc=1, device_id=(lax.rem(opt + k, 128), x), device_id_type=MESH)
        return carry

    lax.fori_loop(1, 128, greet, 0)
    for other in near:
        pl.semaphore_signal(barrier, inc=1, device_id=(opt, other), device_id_type=MESH)
    pl.semaphore_wait(barrier, 129)

    columns = [ahead(z, turn) * 2 for turn in TURNS]

    def send(src, dst, sent, landed, d, place):
        def start():
            pltpu.make_async_remote_copy(
                src.at[d], dst.at[opt], sent, landed, device_id=(d, x), device_id_type=MESH
            ).start()

        if place == 7:
            pl.when(d != opt)(start)
        else:
            start()

    def give(k, carry):
        row = ahead(y, turn_of(lax.rem(k, 8))) * 16 + k // 8
        for place, column in enumerate(columns):
            send(m_ref, inb, in_send, in_recv, row + column, place)
        return carry

    lax.fori_loop(0, 16, give, 0)

    pltpu.make_async_copy(inb.at[pl.ds(0, 127)], inb.at[pl.ds(0, 127)], in_recv).wait()
    pltpu.make_async_copy(inb.at[0], inb.at[0], own).wait()

    def lay(i, carry):
        rows = inb[pl.ds(i * 8, 8)].astype(jnp.float32).reshape(64, 512)
        mat[pl.ds(pl.multiple_of(i * 64, 64), 64), :] = rows.astype(jnp.bfloat16)
        return carry

    lax.fori_loop(0, 16, lay, 0)

    def gram(lo, hi, start):
        return lax.dot_general(mat[:, lo:hi], mat[:, start:], (((0,), (0,)), ((), ())), preferred_element_type=jnp.float32)

    top = gram(0, 256, 0)
    g[0, :, 0:512] = top[0:128]
    g[1, :, 0:384] = top[128:256, 128:]
    low = gram(256, 512, 256)
    g[1, :, 384:640] = low[0:128]
    g[0, :, 512:640] = low[128:256, 128:]

    def exchange(src, dst, stage, half):
        other = near[(stage + half) % 2]
        return pltpu.make_async_remote_copy(
            src.at[half], dst.at[half], x_send.at[stage, half], x_recv.at[stage, half],
            device_id=(opt, other), device_id_type=MESH,
        )

    for half in range(2):
        exchange(g, ra, 0, half).start()

    for half in range(2):
        exchange(g, ra, 0, half).wait_recv()
        g2[half] = g[half] + ra[half]
        exchange(g2, rb, 1, half).start()
    for half in range(2):
        exchange(g2, rb, 1, half).wait_recv()

    where = {0: (0, 0), 1: (1, 0), 2: (1, 384), 3: (0, 512)}

    def block(i, j):
        half, base = where[i]
        cols = slice(base + (j - i) * B, base + (j - i + 1) * B)
        return g2[half, :, cols] + rb[half, :, cols]

    eye = unit(B, B, 0)
    diagonal = jnp.zeros((B, B), jnp.float32)
    for i in range(4):
        for j in range(i, 4):
            blk = block(i, j)
            cur[i * B:(i + 1) * B, j * B:(j + 1) * B] = blk
            if i == j:
                diagonal = diagonal + blk * eye
            else:
                cur[j * B:(j + 1) * B, i * B:(i + 1) * B] = blk.T
    trace = jnp.sum(jnp.sum(diagonal, axis=0, keepdims=True), axis=1, keepdims=True) + epsilon
    scale = 1.0 / trace
    for j in range(2):
        cols = pl.ds(j * 256, 256)
        value = cur[:, cols] * scale
        cur[:, cols] = value
        split(value, cs, cols)

    def poly(panel, cols, start):
        value = first_coef * unit(512, 256, start) + second_coef * cur[:, cols] + third_coef * panel
        split(value, ps, cols)
        return value

    def keep_current(panel, cols, start):
        cur[:, cols] = panel
        split(panel, cs, cols)

    product(cs, cs, poly)
    product(cs, ps, lambda v, cols, start: split(v, qs, cols))
    product(qs, ps, keep_current)
    for h in range(2):
        acs[h] = ps[h]
    product(cs, cs, poly)
    product(acs, ps, lambda v, cols, start: split(v, acs2(acs), cols))
    product(cs, ps, lambda v, cols, start: split(v, qs, cols))
    product(qs, ps, keep_current)
    product(cs, cs, poly)
    root = jnp.sqrt((layers * 1024) / trace)

    def last(v, cols, start):
        fac[:, cols] = (v * root).astype(jnp.bfloat16)

    product(acs2(acs), ps, last)

    def update(i, carry):
        rows = mat[pl.ds(pl.multiple_of(i * 256, 256), 256), :]
        upd[pl.ds(i * 32, 32)] = dot(rows, fac[...]).reshape(32, 8, 512).astype(jnp.bfloat16)
        return carry

    lax.fori_loop(0, 4, update, 0)

    pltpu.make_async_copy(upd.at[opt], ub.at[opt], own).start()

    def give_back(k, carry):
        row = ahead(y, turn_of(k)) * 16
        for place, column in enumerate(columns):
            for core in range(2):
                send(upd, ub, out_send, out_recv, row + column + core, place)
        return carry

    lax.fori_loop(0, 8, give_back, 0)

    for half in range(2):
        exchange(g, ra, 0, half).wait_send()
        exchange(g2, rb, 1, half).wait_send()
    others = pl.ds(0, 127)
    pltpu.make_async_copy(inb.at[others], inb.at[others], in_send).wait()
    pltpu.make_async_copy(upd.at[others], upd.at[others], out_send).wait()
    pltpu.make_async_copy(ub.at[others], ub.at[others], out_recv).wait()
    pltpu.make_async_copy(upd.at[0], upd.at[0], own).wait()


class acs2:
    def __init__(self, ref):
        self.ref = ref
        self.shape = ref.shape

    def __getitem__(self, at):
        at = at if isinstance(at, tuple) else (at,)
        return self.ref[(at[0] + 2, *at[1:])]

    def __setitem__(self, at, value):
        self.ref[(at[0] + 2, *at[1:])] = value


def on_device(momentum, weights):
    places = (128, 8, 512)
    bf, f4 = jnp.bfloat16, jnp.float32
    update = pl.pallas_call(
        step_kernel,
        name="orthogonal_update",
        out_shape=jax.ShapeDtypeStruct(places, bf),
        in_specs=[pl.BlockSpec(memory_space=pltpu.HBM)],
        out_specs=pl.BlockSpec(memory_space=pl.ANY),
        scratch_shapes=[
            *[pltpu.VMEM(places, bf)] * 2,
            pltpu.VMEM((1024, 512), bf),
            *[pltpu.VMEM((2, B, 640), f4)] * 4,
            pltpu.VMEM((512, 512), f4),
            *[pltpu.VMEM((2, 512, 512), bf)] * 3,
            pltpu.VMEM((4, 512, 512), bf),
            pltpu.VMEM((512, 512), bf),
            DMA, DMA, DMA, DMA((2, 2)), DMA((2, 2)), DMA, DMA,
        ],
        compiler_params=pltpu.CompilerParams(collective_id=0, has_side_effects=True, vmem_limit_bytes=24 * 2**20),
    )(momentum.reshape(places))
    update = update.reshape(weights.shape).astype(jnp.float32)
    return (shrink * weights.astype(jnp.float32) - step_rate * update).astype(jnp.bfloat16)


def solution(mesh):
    spec = P("layer", None, "opt", None)
    return jax.shard_map(on_device, mesh=mesh, in_specs=(spec, spec), out_specs=spec, check_vma=False)
```

```python
import functools

import jax
import jax.numpy as jnp
from jax import lax
from jax.experimental import pallas as pl
from jax.experimental.pallas import tpu as pltpu
from jax.sharding import PartitionSpec as P

ITERS = 3
MESH = pl.DeviceIdType.MESH
DMA = pltpu.SemaphoreType.DMA

first_coef = 3.4445
second_coef = -4.775
third_coef = 2.0315
epsilon = 1e-06
step_rate = 0.5
decay_rate = 0.1
shrink = 1.0 - step_rate * decay_rate

B = 128


TURNS = (4, 5, 3, 6, 2, 7, 1, 0)


def turn_of(k):
    half = (8 - k) // 2
    return jnp.where(lax.rem(k, 2) == 1, 8 - half, half)


def ahead(at, turn):
    there = at + turn
    return jnp.where(there >= 8, there - 8, there)


def dot(a, b):
    return jnp.dot(a, b, preferred_element_type=jnp.float32)


def split(value, ref, cols):
    high = value.astype(jnp.bfloat16)
    ref[0, :, cols] = high
    ref[1, :, cols] = (value - high.astype(jnp.float32)).astype(jnp.bfloat16)


def product(a_ref, b_ref, finish, width=256):
    n = a_ref.shape[1]
    left = jnp.concatenate([a_ref[0], a_ref[1], a_ref[0]], axis=1)
    for j in range(n // width):
        cols = pl.ds(j * width, width)
        right = jnp.concatenate([b_ref[0, :, cols], b_ref[0, :, cols], b_ref[1, :, cols]], axis=0)
        finish(dot(left, right), cols, j * width)


def unit(rows, width, start):
    r = lax.broadcasted_iota(jnp.int32, (rows, width), 0)
    c = lax.broadcasted_iota(jnp.int32, (rows, width), 1)
    return (r == c + start).astype(jnp.float32)


def step_kernel(m_ref, ub, inb, upd, mat, g, ra, g2, rb, cur, cs, ps, qs, acs, fac,
                own, in_send, in_recv, x_send, x_recv, out_send, out_recv):
    opt, x = lax.axis_index("opt"), lax.axis_index("layer")
    layers = 4
    chip, c = opt // 2, lax.rem(opt, 2)
    y, z = chip // 8, lax.rem(chip, 8)
    near = (x + 1 - 2 * lax.rem(x, 2), layers - 1 - x)

    pltpu.make_async_copy(m_ref.at[opt], inb.at[opt], own).start()

    columns = [ahead(z, turn) * 2 for turn in TURNS]
    barrier = pltpu.get_barrier_semaphore()

    def greet(k, carry):
        row = ahead(y, turn_of(k)) * 16
        for place, column in enumerate(columns):
            for core in range(2):
                def signal(d=row + column + core):
                    pl.semaphore_signal(barrier, inc=1, device_id=(d, x), device_id_type=MESH)

                if place == 7:
                    pl.when(row + column + core != opt)(signal)
                else:
                    signal()
        return carry

    lax.fori_loop(0, 8, greet, 0)
    for other in near:
        pl.semaphore_signal(barrier, inc=1, device_id=(opt, other), device_id_type=MESH)
    pl.semaphore_wait(barrier, 129)

    def send(src, dst, sent, landed, d, place):
        def start():
            pltpu.make_async_remote_copy(
                src.at[d], dst.at[opt], sent, landed, device_id=(d, x), device_id_type=MESH
            ).start()

        if place == 7:
            pl.when(d != opt)(start)
        else:
            start()

    def give(k, carry):
        row = ahead(y, turn_of(lax.rem(k, 8))) * 16 + k // 8
        for place, column in enumerate(columns):
            send(m_ref, inb, in_send, in_recv, row + column, place)
        return carry

    lax.fori_loop(0, 16, give, 0)

    pltpu.make_async_copy(inb.at[pl.ds(0, 127)], inb.at[pl.ds(0, 127)], in_recv).wait()
    pltpu.make_async_copy(inb.at[0], inb.at[0], own).wait()

    def lay(i, carry):
        rows = inb[pl.ds(i * 8, 8)].astype(jnp.float32).reshape(64, 512)
        mat[pl.ds(pl.multiple_of(i * 64, 64), 64), :] = rows.astype(jnp.bfloat16)
        return carry

    lax.fori_loop(0, 16, lay, 0)

    def gram(lo, hi, start):
        return lax.dot_general(mat[:, lo:hi], mat[:, start:], (((0,), (0,)), ((), ())), preferred_element_type=jnp.float32)

    top = gram(0, 256, 0)
    g[0, :, 0:512] = top[0:128]
    g[1, :, 0:384] = top[128:256, 128:]
    low = gram(256, 512, 256)
    g[1, :, 384:640] = low[0:128]
    g[0, :, 512:640] = low[128:256, 128:]

    def exchange(src, dst, stage, part, half):
        rows = pl.ds(part * 64, 64)
        return pltpu.make_async_remote_copy(
            src.at[half, rows], dst.at[half, rows],
            x_send.at[stage, half, part], x_recv.at[stage, half, part],
            device_id=(opt, near[(stage + half) % 2]), device_id_type=MESH,
        )

    pieces = [(part, half) for part in range(2) for half in range(2)]
    for piece in pieces:
        exchange(g, ra, 0, *piece).start()
    for part, half in pieces:
        rows = pl.ds(part * 64, 64)
        exchange(g, ra, 0, part, half).wait_recv()
        g2[half, rows] = g[half, rows] + ra[half, rows]
        exchange(g2, rb, 1, part, half).start()
    for piece in pieces:
        exchange(g2, rb, 1, *piece).wait_recv()

    where = {0: (0, 0), 1: (1, 0), 2: (1, 384), 3: (0, 512)}

    def block(i, j):
        half, base = where[i]
        cols = slice(base + (j - i) * B, base + (j - i + 1) * B)
        return g2[half, :, cols] + rb[half, :, cols]

    eye = unit(B, B, 0)
    diagonal = jnp.zeros((B, B), jnp.float32)
    for i in range(4):
        for j in range(i, 4):
            blk = block(i, j)
            cur[i * B:(i + 1) * B, j * B:(j + 1) * B] = blk
            if i == j:
                diagonal = diagonal + blk * eye
            else:
                cur[j * B:(j + 1) * B, i * B:(i + 1) * B] = blk.T
    trace = jnp.sum(jnp.sum(diagonal, axis=0, keepdims=True), axis=1, keepdims=True) + epsilon
    scale = 1.0 / trace
    for j in range(2):
        cols = pl.ds(j * 256, 256)
        value = cur[:, cols] * scale
        cur[:, cols] = value
        split(value, cs, cols)

    def poly(panel, cols, start):
        value = first_coef * unit(512, 256, start) + second_coef * cur[:, cols] + third_coef * panel
        split(value, ps, cols)
        return value

    def keep_current(panel, cols, start):
        cur[:, cols] = panel
        split(panel, cs, cols)

    product(cs, cs, poly)
    product(cs, ps, lambda v, cols, start: split(v, qs, cols))
    product(qs, ps, keep_current)
    for h in range(2):
        acs[h] = ps[h]
    product(cs, cs, poly)
    product(acs, ps, lambda v, cols, start: split(v, acs2(acs), cols))
    product(cs, ps, lambda v, cols, start: split(v, qs, cols))
    product(qs, ps, keep_current)
    product(cs, cs, poly)
    root = jnp.sqrt((layers * 1024) / trace)

    def last(v, cols, start):
        fac[:, cols] = (v * root).astype(jnp.bfloat16)

    product(acs2(acs), ps, last)

    def update(i, carry):
        rows = mat[pl.ds(pl.multiple_of(i * 256, 256), 256), :]
        upd[pl.ds(i * 32, 32)] = dot(rows, fac[...]).reshape(32, 8, 512).astype(jnp.bfloat16)
        return carry

    lax.fori_loop(0, 4, update, 0)

    pltpu.make_async_copy(upd.at[opt], ub.at[opt], own).start()

    def give_back(k, carry):
        row = ahead(y, turn_of(k)) * 16
        for place, column in enumerate(columns):
            for core in range(2):
                send(upd, ub, out_send, out_recv, row + column + core, place)
        return carry

    lax.fori_loop(0, 8, give_back, 0)

    for piece in pieces:
        exchange(g, ra, 0, *piece).wait_send()
        exchange(g2, rb, 1, *piece).wait_send()
    others = pl.ds(0, 127)
    pltpu.make_async_copy(inb.at[others], inb.at[others], in_send).wait()
    pltpu.make_async_copy(upd.at[others], upd.at[others], out_send).wait()
    pltpu.make_async_copy(ub.at[others], ub.at[others], out_recv).wait()
    pltpu.make_async_copy(upd.at[0], upd.at[0], own).wait()


class acs2:
    def __init__(self, ref):
        self.ref = ref
        self.shape = ref.shape

    def __getitem__(self, at):
        at = at if isinstance(at, tuple) else (at,)
        return self.ref[(at[0] + 2, *at[1:])]

    def __setitem__(self, at, value):
        self.ref[(at[0] + 2, *at[1:])] = value


def on_device(momentum, weights):
    places = (128, 8, 512)
    bf, f4 = jnp.bfloat16, jnp.float32
    update = pl.pallas_call(
        step_kernel,
        name="orthogonal_update",
        out_shape=jax.ShapeDtypeStruct(places, bf),
        in_specs=[pl.BlockSpec(memory_space=pltpu.HBM)],
        out_specs=pl.BlockSpec(memory_space=pl.ANY),
        scratch_shapes=[
            *[pltpu.VMEM(places, bf)] * 2,
            pltpu.VMEM((1024, 512), bf),
            *[pltpu.VMEM((2, B, 640), f4)] * 4,
            pltpu.VMEM((512, 512), f4),
            *[pltpu.VMEM((2, 512, 512), bf)] * 3,
            pltpu.VMEM((4, 512, 512), bf),
            pltpu.VMEM((512, 512), bf),
            DMA, DMA, DMA, DMA((2, 2, 2)), DMA((2, 2, 2)), DMA, DMA,
        ],
        compiler_params=pltpu.CompilerParams(collective_id=0, has_side_effects=True, vmem_limit_bytes=24 * 2**20),
    )(pltpu.with_memory_space_constraint(momentum.reshape(places), pltpu.HBM))
    update = update.reshape(weights.shape).astype(jnp.float32)
    return (shrink * weights.astype(jnp.float32) - step_rate * update).astype(jnp.bfloat16)


def solution(mesh):
    spec = P("layer", None, "opt", None)
    return jax.shard_map(on_device, mesh=mesh, in_specs=(spec, spec), out_specs=spec, check_vma=False)
```

```python
import functools

import jax
import jax.numpy as jnp
from jax import lax
from jax.experimental import pallas as pl
from jax.experimental.pallas import tpu as pltpu
from jax.sharding import PartitionSpec as P

ITERS = 3
MESH = pl.DeviceIdType.MESH
DMA = pltpu.SemaphoreType.DMA

first_coef = 3.4445
second_coef = -4.775
third_coef = 2.0315
epsilon = 1e-06
step_rate = 0.5
decay_rate = 0.1
shrink = 1.0 - step_rate * decay_rate

B = 128


TURNS = (4, 5, 3, 6, 2, 7, 1, 0)


def turn_of(k):
    half = (8 - k) // 2
    return jnp.where(lax.rem(k, 2) == 1, 8 - half, half)


def ahead(at, turn):
    there = at + turn
    return jnp.where(there >= 8, there - 8, there)


def dot(a, b):
    return jnp.dot(a, b, preferred_element_type=jnp.float32)


def split(value, ref, cols):
    high = value.astype(jnp.bfloat16)
    ref[0, :, cols] = high
    ref[1, :, cols] = (value - high.astype(jnp.float32)).astype(jnp.bfloat16)


def product(a_ref, b_ref, finish, width=256):
    n = a_ref.shape[1]
    left = jnp.concatenate([a_ref[0], a_ref[1], a_ref[0]], axis=1)
    for j in range(n // width):
        cols = pl.ds(j * width, width)
        right = jnp.concatenate([b_ref[0, :, cols], b_ref[0, :, cols], b_ref[1, :, cols]], axis=0)
        finish(dot(left, right), cols, j * width)


def unit(rows, width, start):
    r = lax.broadcasted_iota(jnp.int32, (rows, width), 0)
    c = lax.broadcasted_iota(jnp.int32, (rows, width), 1)
    return (r == c + start).astype(jnp.float32)


def step_kernel(m_ref, ub, inb, upd, mat, g, ra, g2, rb, cur, cs, ps, qs, acs, fac,
                own, in_send, in_recv, x_send, x_recv, out_send, out_recv):
    opt, x = lax.axis_index("opt"), lax.axis_index("layer")
    layers = 4
    chip, c = opt // 2, lax.rem(opt, 2)
    y, z = chip // 8, lax.rem(chip, 8)
    near = (x + 1 - 2 * lax.rem(x, 2), layers - 1 - x)

    pltpu.make_async_copy(m_ref.at[opt], inb.at[opt], own).start()

    columns = [ahead(z, turn) * 2 for turn in TURNS]
    barrier = pltpu.get_barrier_semaphore()

    def greet(k, carry):
        row = ahead(y, turn_of(k)) * 16
        for place, column in enumerate(columns):
            for core in range(2):
                def signal(d=row + column + core):
                    pl.semaphore_signal(barrier, inc=1, device_id=(d, x), device_id_type=MESH)

                if place == 7:
                    pl.when(row + column + core != opt)(signal)
                else:
                    signal()
        return carry

    lax.fori_loop(0, 8, greet, 0)
    for other in near:
        pl.semaphore_signal(barrier, inc=1, device_id=(opt, other), device_id_type=MESH)
    pl.semaphore_wait(barrier, 129)

    def send(src, dst, sent, landed, d, place):
        def start():
            pltpu.make_async_remote_copy(
                src.at[d], dst.at[opt], sent, landed, device_id=(d, x), device_id_type=MESH
            ).start()

        if place == 7:
            pl.when(d != opt)(start)
        else:
            start()

    def give(k, carry):
        row = ahead(y, turn_of(lax.rem(k, 8))) * 16 + k // 8
        for place, column in enumerate(columns):
            send(m_ref, inb, in_send, in_recv, row + column, place)
        return carry

    lax.fori_loop(0, 16, give, 0)

    pltpu.make_async_copy(inb.at[pl.ds(0, 127)], inb.at[pl.ds(0, 127)], in_recv).wait()
    pltpu.make_async_copy(inb.at[0], inb.at[0], own).wait()

    def lay(i, carry):
        rows = inb[pl.ds(i * 8, 8)].astype(jnp.float32).reshape(64, 512)
        mat[pl.ds(pl.multiple_of(i * 64, 64), 64), :] = rows.astype(jnp.bfloat16)
        return carry

    lax.fori_loop(0, 16, lay, 0)

    def gram(lo, hi, start):
        return lax.dot_general(mat[:, lo:hi], mat[:, start:], (((0,), (0,)), ((), ())), preferred_element_type=jnp.float32)

    top = gram(0, 256, 0)
    g[0, :, 0:512] = top[0:128]
    g[1, :, 0:384] = top[128:256, 128:]
    low = gram(256, 512, 256)
    g[1, :, 384:640] = low[0:128]
    g[0, :, 512:640] = low[128:256, 128:]

    def exchange(src, dst, stage, part, half):
        rows = pl.ds(part * 64, 64)
        return pltpu.make_async_remote_copy(
            src.at[half, rows], dst.at[half, rows],
            x_send.at[stage, half, part], x_recv.at[stage, half, part],
            device_id=(opt, near[(stage + half) % 2]), device_id_type=MESH,
        )

    pieces = [(part, half) for part in range(2) for half in range(2)]
    for piece in pieces:
        exchange(g, ra, 0, *piece).start()
    for part, half in pieces:
        rows = pl.ds(part * 64, 64)
        exchange(g, ra, 0, part, half).wait_recv()
        g2[half, rows] = g[half, rows] + ra[half, rows]
        exchange(g2, rb, 1, part, half).start()
    for piece in pieces:
        exchange(g2, rb, 1, *piece).wait_recv()

    where = {0: (0, 0), 1: (1, 0), 2: (1, 384), 3: (0, 512)}

    def block(i, j):
        half, base = where[i]
        cols = slice(base + (j - i) * B, base + (j - i + 1) * B)
        return g2[half, :, cols] + rb[half, :, cols]

    eye = unit(B, B, 0)
    diagonal = jnp.zeros((B, B), jnp.float32)
    for i in range(4):
        for j in range(i, 4):
            blk = block(i, j)
            cur[i * B:(i + 1) * B, j * B:(j + 1) * B] = blk
            if i == j:
                diagonal = diagonal + blk * eye
            else:
                cur[j * B:(j + 1) * B, i * B:(i + 1) * B] = blk.T
    trace = jnp.sum(jnp.sum(diagonal, axis=0, keepdims=True), axis=1, keepdims=True) + epsilon
    scale = 1.0 / trace
    for j in range(2):
        cols = pl.ds(j * 256, 256)
        value = cur[:, cols] * scale
        cur[:, cols] = value
        split(value, cs, cols)

    def poly(panel, cols, start):
        value = first_coef * unit(512, 256, start) + second_coef * cur[:, cols] + third_coef * panel
        split(value, ps, cols)
        return value

    def keep_current(panel, cols, start):
        cur[:, cols] = panel
        split(panel, cs, cols)

    product(cs, cs, poly)
    product(cs, ps, lambda v, cols, start: split(v, qs, cols))
    product(qs, ps, keep_current)
    for h in range(2):
        acs[h] = ps[h]
    product(cs, cs, poly)
    product(acs, ps, lambda v, cols, start: split(v, acs2(acs), cols))
    product(cs, ps, lambda v, cols, start: split(v, qs, cols))
    product(qs, ps, keep_current)
    product(cs, cs, poly)
    root = jnp.sqrt((layers * 1024) / trace)

    def last(v, cols, start):
        fac[:, cols] = (v * root).astype(jnp.bfloat16)

    product(acs2(acs), ps, last)

    def update(i, carry):
        rows = mat[pl.ds(pl.multiple_of(i * 256, 256), 256), :]
        upd[pl.ds(i * 32, 32)] = dot(rows, fac[...]).reshape(32, 8, 512).astype(jnp.bfloat16)
        return carry

    lax.fori_loop(0, 4, update, 0)

    pltpu.make_async_copy(upd.at[opt], ub.at[opt], own).start()

    def give_back(k, carry):
        for place, column in enumerate(columns):
            row = ahead(y, turn_of(lax.rem(k + place, 8))) * 16
            for core in range(2):
                send(upd, ub, out_send, out_recv, row + column + core, place)
        return carry

    lax.fori_loop(0, 8, give_back, 0)

    for piece in pieces:
        exchange(g, ra, 0, *piece).wait_send()
        exchange(g2, rb, 1, *piece).wait_send()
    others = pl.ds(0, 127)
    pltpu.make_async_copy(inb.at[others], inb.at[others], in_send).wait()
    pltpu.make_async_copy(upd.at[others], upd.at[others], out_send).wait()
    pltpu.make_async_copy(ub.at[others], ub.at[others], out_recv).wait()
    pltpu.make_async_copy(upd.at[0], upd.at[0], own).wait()


class acs2:
    def __init__(self, ref):
        self.ref = ref
        self.shape = ref.shape

    def __getitem__(self, at):
        at = at if isinstance(at, tuple) else (at,)
        return self.ref[(at[0] + 2, *at[1:])]

    def __setitem__(self, at, value):
        self.ref[(at[0] + 2, *at[1:])] = value


def on_device(momentum, weights):
    places = (128, 8, 512)
    bf, f4 = jnp.bfloat16, jnp.float32
    update = pl.pallas_call(
        step_kernel,
        name="orthogonal_update",
        out_shape=jax.ShapeDtypeStruct(places, bf),
        in_specs=[pl.BlockSpec(memory_space=pltpu.HBM)],
        out_specs=pl.BlockSpec(memory_space=pl.ANY),
        scratch_shapes=[
            *[pltpu.VMEM(places, bf)] * 2,
            pltpu.VMEM((1024, 512), bf),
            *[pltpu.VMEM((2, B, 640), f4)] * 4,
            pltpu.VMEM((512, 512), f4),
            *[pltpu.VMEM((2, 512, 512), bf)] * 3,
            pltpu.VMEM((4, 512, 512), bf),
            pltpu.VMEM((512, 512), bf),
            DMA, DMA, DMA, DMA((2, 2, 2)), DMA((2, 2, 2)), DMA, DMA,
        ],
        compiler_params=pltpu.CompilerParams(collective_id=0, has_side_effects=True, vmem_limit_bytes=24 * 2**20),
    )(pltpu.with_memory_space_constraint(momentum.reshape(places), pltpu.HBM))
    update = update.reshape(weights.shape).astype(jnp.float32)
    return (shrink * weights.astype(jnp.float32) - step_rate * update).astype(jnp.bfloat16)


def solution(mesh):
    spec = P("layer", None, "opt", None)
    return jax.shard_map(on_device, mesh=mesh, in_specs=(spec, spec), out_specs=spec, check_vma=False)
```
